32 devices in a mesh: group: 4 (over y, core), dom: 8 (over z, x).
Axes of the slice: x: 2, y: 2, z: 4, core: 2. Of those that a mesh axis runs over, the one named last changes fastest.
Arguments:
- features: float32 [4096, 1024], P(('group', 'dom')), may hold values from -6 to 6
- known_mask: int32 [4096], P(('group', 'dom')), may hold values 0 or 1
- local_tile: bfloat16 [4096, 128], P(('group', 'dom')), may hold values from 0 to 1.5, as said below
- peer_tile: bfloat16 [4096, 256], P(('group', 'dom')), may hold values from 0 to 1.5, as said below
- cross_tile: bfloat16 [4096, 128], P(('group', 'dom')), may hold values from 0 to 1.5, as said below
- peer_rows: int32 [4, 8, 8, 32], P('group', 'dom'), may hold values from 0 to 127
- cross_rows: int32 [4, 8, 4, 32], P('group', 'dom'), may hold values from 0 to 127
- labels: int32 [4096], P(('group', 'dom')), may hold values from 0 to 18
- first_weight: bfloat16 [1024, 1024], replicated, may hold values from -0.1875 to 0.1875
- first_bias: float32 [1024], replicated, may hold values from -3 to 3
- second_weight: bfloat16 [1024, 19], replicated, may hold values from -60 to 60
- second_bias: float32 [19], replicated, may hold values from -3 to 3
Outputs:
- imputed: float32 [4096, 1024], P(('group', 'dom'))
- grad_first: float32 [1024, 1024], P('dom')
- grad_first_bias: float32 [1024], replicated
- grad_second: float32 [1024, 19], replicated
- grad_second_bias: float32 [19], replicated
The draws below stay inside these ranges and needn't reach their ends.
Inputs may be any that keep to these rules, and one draw needn't show every extreme that they name: `local_tile`: each entry is 0 or lies in 0.5 to 1.5; a fraction of about 8 / 128 is nonzero. `peer_tile`: each entry is 0 or lies in 0.5 to 1.5; a fraction of about 6 / 256 is nonzero. `cross_tile`: each entry is 0 or lies in 0.5 to 1.5; a fraction of about 4 / 128 is nonzero.
All inputs are finite; a program needn't handle non-finite values. No bound on the sum of `known_mask` on one device may be relied on, other than what follows from the above.
Results may differ from the reference program's by a relative error of at most 0.0041.
Values sent between devices are 32-bit elements; how exact they have to be, the bound alone decides.
A program may use at most 64 MiB of HBM per device.

```python
import jax
import jax.numpy as jnp
from jax import lax

FEAT = 1024
UNITS = 1024
CLASSES = 19
ROWS = 128
HALO_DEV = 256
CROSS_DEV = 128
SWEEPS = 3
PEER_SLOTS = 32
CROSS_SLOTS = 32
NODES = 4096
N_GROUP = 4
N_DOM = 8


def sparse_tile(key, height, width, density):
    chosen = jax.random.uniform(jax.random.fold_in(key, 11), (height, width), dtype=jnp.float32) < density
    values = jax.random.uniform(jax.random.fold_in(key, 12), (height, width), dtype=jnp.float32, minval=0.5, maxval=1.5)
    return jnp.where(chosen, values, jnp.float32(0.0)).astype(jnp.bfloat16)


def draw_local_tile(key, part):
    return sparse_tile(key, NODES, ROWS, min(1.0, 8.0 / ROWS))


def draw_peer_tile(key, part):
    return sparse_tile(jax.random.fold_in(key, 21), NODES, HALO_DEV, min(1.0, 6.0 / HALO_DEV))


def draw_cross_tile(key, part):
    return sparse_tile(jax.random.fold_in(key, 31), NODES, CROSS_DEV, min(1.0, 4.0 / CROSS_DEV))


def draw_second_weight(key, part):
    normal = jax.random.normal(jax.random.fold_in(key, 41), (UNITS, CLASSES), dtype=jnp.float32)
    values = jnp.clip(normal / jnp.sqrt(jnp.float32(UNITS)), -60.0, 60.0)
    return values.astype(jnp.bfloat16)


def place_ends(values, rng, least, top_value):
    place = [jax.random.randint(jax.random.fold_in(rng, axis), (), 0, length) for axis, length in enumerate(values.shape)]
    main_axis = values.shape.index(max(values.shape))
    next_to = place[:main_axis] + [(place[main_axis] + 1) % values.shape[main_axis]] + place[main_axis + 1:]
    return values.at[tuple(place)].set(least).at[tuple(next_to)].set(top_value)


def steps_of(key, shape, shards, least, high):
    def one(dim, blocks):
        draws = jax.random.uniform(jax.random.fold_in(jax.random.fold_in(key, 6), dim), (blocks,), jnp.float32, least / len(shards), high / len(shards))
        return jnp.repeat(jnp.exp(draws), shape[dim] // blocks).reshape((-1,) + (1,) * (len(shape) - dim - 1))

    loudness = one(*shards[0])
    for cut in shards[1:]:
        loudness = loudness * one(*cut)
    return loudness


def gaussian(own_key, shape, deviation, most, cuts=(), kind=jnp.bfloat16):
    result = jax.random.normal(own_key, shape, jnp.float32) * deviation
    if len(cuts) > 0:
        result = steps_of(own_key, shape, cuts, -0.22, 0.18) * result
    return jnp.clip(result, min=-most, max=most).astype(kind)


def setup_inputs(seed: int = 0) -> dict:
    seeds = jax.random.split(jax.random.key(seed), 13)
    return {
        "features": gaussian(seeds[0], (NODES, FEAT), 1.0, 6.0, ((0, 32),), jnp.float32),
        "known_mask": place_ends((jax.random.randint(seeds[1], (NODES,), 0, 5) < 2).astype(jnp.int32), jax.random.fold_in(seeds[1], 1), 0, 1),
        "local_tile": draw_local_tile(jax.random.fold_in(seeds[12], 71), 0),
        "peer_tile": draw_peer_tile(jax.random.fold_in(seeds[12], 71), 0),
        "cross_tile": draw_cross_tile(jax.random.fold_in(seeds[12], 71), 0),
        "peer_rows": place_ends(jax.random.randint(seeds[5], (N_GROUP, N_DOM, N_DOM, PEER_SLOTS), 0, ROWS), jax.random.fold_in(seeds[5], 1), 0, ROWS - 1).astype(jnp.int32),
        "cross_rows": place_ends(jax.random.randint(seeds[6], (N_GROUP, N_DOM, N_GROUP, CROSS_SLOTS), 0, ROWS), jax.random.fold_in(seeds[6], 1), 0, ROWS - 1).astype(jnp.int32),
        "labels": place_ends(jax.random.randint(seeds[7], (NODES,), 0, CLASSES), jax.random.fold_in(seeds[7], 1), 0, CLASSES - 1).astype(jnp.int32),
        "first_weight": gaussian(seeds[8], (FEAT, UNITS), FEAT ** -0.5, 0.1875),
        "first_bias": gaussian(seeds[9], (UNITS,), 0.5, 3.0, (), jnp.float32),
        "second_weight": draw_second_weight(jax.random.fold_in(seeds[12], 71), 0),
        "second_bias": gaussian(seeds[11], (CLASSES,), 0.5, 3.0, (), jnp.float32),
    }


def reference(features, known_mask, local_tile, peer_tile, cross_tile, peer_rows, cross_rows, labels, first_weight, first_bias, second_weight, second_bias):
    highest = lax.Precision.HIGHEST
    keep = (known_mask == 1)[:, None]
    current = jnp.where(keep, features, jnp.float32(0.0))
    local_full = local_tile.astype(jnp.float32)
    peer_full = peer_tile.astype(jnp.float32)
    cross_full = cross_tile.astype(jnp.float32)
    degree = 1.0 + lax.optimization_barrier(jnp.sum(local_full, axis=1)) + lax.optimization_barrier(jnp.sum(peer_full, axis=1)) + lax.optimization_barrier(jnp.sum(cross_full, axis=1))
    degree = degree[:, None]
    local_four = local_full.reshape(N_GROUP, N_DOM, ROWS, ROWS)
    peer_four = peer_full.reshape(N_GROUP, N_DOM, ROWS, HALO_DEV)
    cross_four = cross_full.reshape(N_GROUP, N_DOM, ROWS, CROSS_DEV)
    dom_index = jnp.arange(N_DOM, dtype=jnp.int32)
    group_range = jnp.arange(N_GROUP, dtype=jnp.int32)
    for sweep in range(SWEEPS):
        grid = current.reshape(N_GROUP, N_DOM, ROWS, FEAT)

        def one_group(group_index):
            group_rows = grid[group_index]
            listed = jnp.transpose(peer_rows[group_index], (1, 0, 2))
            peer_halo = group_rows[dom_index[None, :, None], listed].reshape(N_DOM, HALO_DEV, FEAT)
            cross_list = cross_rows[:, :, group_index, :]
            cross_halo = grid[group_range[:, None, None], dom_index[None, :, None], cross_list]
            cross_halo = jnp.transpose(cross_halo, (1, 0, 2, 3)).reshape(N_DOM, CROSS_DEV, FEAT)
            summed = group_rows + jnp.einsum('prk,pkf->prf', local_four[group_index], group_rows, precision=highest)
            summed = summed + jnp.einsum('prk,pkf->prf', peer_four[group_index], peer_halo, precision=highest)
            summed = summed + jnp.einsum('prk,pkf->prf', cross_four[group_index], cross_halo, precision=highest)
            return summed
        summed = lax.map(one_group, group_range).reshape(NODES, FEAT)
        current = jnp.where(keep, features, summed / degree)
    imputed = current
    inputs = imputed.astype(jnp.bfloat16)
    pre = jnp.dot(inputs, first_weight, preferred_element_type=jnp.float32) + first_bias
    sigma = jax.nn.sigmoid(pre)
    active = (pre * sigma).astype(jnp.bfloat16)
    logits = jnp.dot(active, second_weight, preferred_element_type=jnp.float32) + second_bias
    shifted = logits - lax.optimization_barrier(jnp.max(logits, axis=1, keepdims=True))
    expo = jnp.exp(shifted)
    probs = expo / lax.optimization_barrier(jnp.sum(expo, axis=1, keepdims=True))
    onehot = (labels[:, None] == jnp.arange(CLASSES, dtype=jnp.int32)[None, :]).astype(jnp.float32)
    dlogits = (probs - onehot) / jnp.sqrt(jnp.float32(NODES))
    dlogits_b = dlogits.astype(jnp.bfloat16)
    grad_second_bias = lax.optimization_barrier(jnp.sum(dlogits, axis=0))
    grad_second = lax.dot_general(active, dlogits_b, (((0,), (0,)), ((), ())), preferred_element_type=jnp.float32)
    back = lax.dot_general(dlogits_b, second_weight, (((1,), (1,)), ((), ())), preferred_element_type=jnp.float32)
    dpre = (back * sigma * (1.0 + pre * (1.0 - sigma))).astype(jnp.bfloat16)
    grad_first_bias = lax.optimization_barrier(jnp.sum(dpre.astype(jnp.float32), axis=0))
    grad_first = lax.dot_general(inputs, dpre, (((0,), (0,)), ((), ())), preferred_element_type=jnp.float32)
    return (imputed, grad_first, grad_first_bias, grad_second, grad_second_bias)
```

```python
import functools
import math

import jax
import jax.numpy as jnp
from jax import lax
from jax.experimental import pallas as pl
from jax.experimental.pallas import tpu as pltpu
from jax.sharding import PartitionSpec as P

SWEEPS = 3
CHUNKS = 2
MESH = pl.DeviceIdType.MESH


def split(x):
    high = x.astype(jnp.bfloat16)
    low = (x - high.astype(jnp.float32)).astype(jnp.bfloat16)
    return high, low


def two_pass(a, parts):
    out = jnp.dot(a, parts[0], preferred_element_type=jnp.float32)
    return out + jnp.dot(a, parts[1], preferred_element_type=jnp.float32)


def bits_of(name, n):
    return [(name, b) for b in range(n.bit_length() - 1)]


def reduce_orders(n_group, n_dom):
    group, dom = bits_of("group", n_group), bits_of("dom", n_dom)
    bulk_a = group + dom
    bulk_b = group[:1] + dom[:1] + group[1:] + dom[1:]
    small = dom[1:] + group[:1] + dom[:1] + group[1:]
    return [bulk_a, bulk_b], small


def kernel(
    n_group, n_dom, peer_slots, cross_slots, total_nodes,
    feat_ref, keep_ref, local_ref, peer_ref, cross_ref, pick_ref, label_ref,
    w1_hbm, b1_ref, w2_ref, b2_ref,
    imputed_ref, grad_ref, small_ref,
    w1_ref, cur, send, recv, inputs, grads, incoming, small_acc, small_in, gathered,
    w1_sem, send_sem, recv_sem, bulk_send, bulk_recv, small_send, small_recv,
    out_send, out_recv,
):
    sizes = {"group": n_group, "dom": n_dom}
    me = {name: lax.axis_index(name) for name in sizes}
    rows, width = feat_ref.shape
    cols = width // CHUNKS
    peer_total = n_dom * peer_slots

    load_w1 = pltpu.make_async_copy(w1_hbm, w1_ref, w1_sem)
    load_w1.start()
    barrier = pltpu.get_barrier_semaphore()
    for name, n in sizes.items():
        for k in range(1, n):
            pl.semaphore_signal(
                barrier, inc=1, device_id={name: lax.rem(me[name] + k, n)}, device_id_type=MESH
            )

    local = local_ref[...]
    halo = jnp.concatenate([peer_ref[...], cross_ref[...]], axis=1)
    degree = (
        1.0
        + jnp.sum(local.astype(jnp.float32), axis=1, keepdims=True)
        + jnp.sum(halo.astype(jnp.float32), axis=1, keepdims=True)
    )
    keep = keep_ref[...] == 1
    pick = pick_ref[...]

    def exchange(sweep, c, parts):
        out = send.at[sweep, c]
        into = recv.at[sweep, c]
        send[sweep, c] = two_pass(pick, parts)
        for name, base, slots in (("dom", 0, peer_slots), ("group", peer_total, cross_slots)):
            n = sizes[name]
            mine = pl.ds(pl.multiple_of(base + me[name] * slots, slots), slots)
            for k in list(range(1, n)):
                there = lax.rem(me[name] + k, n)
                pltpu.make_async_remote_copy(
                    src_ref=out.at[pl.ds(pl.multiple_of(base + there * slots, slots), slots)],
                    dst_ref=into.at[mine],
                    send_sem=send_sem.at[sweep, c],
                    recv_sem=recv_sem.at[sweep, c],
                    device_id={name: there},
                    device_id_type=MESH,
                ).start()
            pltpu.make_async_copy(out.at[mine], into.at[mine], recv_sem.at[sweep, c]).start()

    for c in range(CHUNKS):
        now = jnp.where(keep, feat_ref[:, c * cols:(c + 1) * cols], jnp.float32(0.0))
        cur[c] = now
        if c == 0:
            pl.semaphore_wait(barrier, n_dom - 1 + n_group - 1)
        exchange(0, c, split(now))
    for sweep in range(SWEEPS):
        for c in range(CHUNKS):
            area = slice(c * cols, (c + 1) * cols)
            now = cur[c]
            summed = now + two_pass(local, split(now))
            pltpu.make_async_copy(
                recv.at[sweep, c], recv.at[sweep, c], recv_sem.at[sweep, c]
            ).wait()
            summed = summed + two_pass(halo, split(recv[sweep, c]))
            now = jnp.where(keep, feat_ref[:, area], summed / degree)
            if sweep + 1 < SWEEPS:
                cur[c] = now
                exchange(sweep + 1, c, split(now))
            else:
                imputed_ref[:, area] = now
                inputs[:, area] = now.astype(jnp.bfloat16)

    load_w1.wait()
    pre = jnp.dot(inputs[...], w1_ref[...], preferred_element_type=jnp.float32) + b1_ref[...]
    sigma = jax.nn.sigmoid(pre)
    active = (pre * sigma).astype(jnp.bfloat16)
    w2 = w2_ref[...]
    logits = jnp.dot(active, w2, preferred_element_type=jnp.float32) + b2_ref[...]
    shifted = logits - jnp.max(logits, axis=1, keepdims=True)
    expo = jnp.exp(shifted)
    probs = expo / jnp.sum(expo, axis=1, keepdims=True)
    classes = w2.shape[1]
    hot = label_ref[...] == lax.broadcasted_iota(jnp.int32, (rows, classes), 1)
    dlogits = (probs - hot.astype(jnp.float32)) / jnp.float32(math.sqrt(total_nodes))
    dlogits_b = dlogits.astype(jnp.bfloat16)
    back = lax.dot_general(
        dlogits_b, w2, (((1,), (1,)), ((), ())), preferred_element_type=jnp.float32
    )
    dpre32 = back * sigma * (1.0 + pre * (1.0 - sigma))
    dpre = dpre32.astype(jnp.bfloat16)

    orders, small_order = reduce_orders(n_group, n_dom)
    stages = len(small_order)

    def bit(name, b):
        return lax.rem(lax.div(me[name], 1 << b), 2)

    def partner(name, b):
        return {name: me[name] + (1 << b) * (1 - 2 * bit(name, b))}

    small_acc[0] = jnp.zeros(small_acc.shape[1:], jnp.float32)
    small_acc[0, :classes] = lax.dot_general(
        dlogits_b, active, (((0,), (0,)), ((), ())), preferred_element_type=jnp.float32
    )
    small_acc[0, classes:classes + 1] = jnp.sum(dpre.astype(jnp.float32), axis=0, keepdims=True)
    small_acc[0, classes + 1:classes + 2, :classes] = jnp.sum(dlogits, axis=0, keepdims=True)

    def small_copy(s):
        return pltpu.make_async_remote_copy(
            src_ref=small_acc.at[s],
            dst_ref=small_in.at[s],
            send_sem=small_send.at[s],
            recv_sem=small_recv.at[s],
            device_id=partner(*small_order[s]),
            device_id_type=MESH,
        )

    deep, share = width // n_dom, width // n_dom // n_group
    blocks = n_group * n_dom

    def place(order, where):
        at = 0
        for name, b in order:
            at = 2 * at + ((where[name] >> b) & 1)
        return at

    start, length, offset = [0] * CHUNKS, blocks, 0
    copies = [[] for _ in range(CHUNKS)]

    def bulk_start(s, h):
        half = blocks >> (s + 1)
        name, b = orders[h][s]
        mine = bit(name, b)
        copy = pltpu.make_async_remote_copy(
            src_ref=grads.at[h, pl.ds(start[h] + (1 - mine) * half, half)],
            dst_ref=incoming.at[h, pl.ds(blocks - 2 * half, half)],
            send_sem=bulk_send.at[h, s],
            recv_sem=bulk_recv.at[h, s],
            device_id=partner(name, b),
            device_id_type=MESH,
        )
        copy.start()
        copies[h].append(copy)
        start[h] = start[h] + mine * half

    small_copies = [small_copy(0)]
    small_copies[0].start()
    for h in range(CHUNKS):
        units = dpre.shape[1] // CHUNKS
        part = dpre[:, h * units:(h + 1) * units]
        for d in range(n_dom):
            term = lax.dot_general(
                inputs[:, d * deep:(d + 1) * deep], part, (((0,), (0,)), ((), ())),
                preferred_element_type=jnp.float32,
            )
            for g in range(n_group):
                grads[h, place(orders[h], {"group": g, "dom": d})] = term[g * share:(g + 1) * share]
        bulk_start(0, h)
    for s in range(stages):
        half = blocks >> (s + 1)
        for h in range(CHUNKS):
            copies[h][s].wait_recv()
            kept = pl.ds(start[h], half)
            grads[h, kept] = grads[h, kept] + incoming[h, pl.ds(blocks - 2 * half, half)]
            if s + 1 < stages:
                bulk_start(s + 1, h)
        small_copies[s].wait_recv()
        small_acc[s + 1] = small_acc[s] + small_in[s]
        if s + 1 < stages:
            small_copies.append(small_copy(s + 1))
            small_copies[-1].start()

    g_me = me["group"]
    for h in range(CHUNKS):
        for k in range(1, n_group):
            pltpu.make_async_remote_copy(
                src_ref=grads.at[h, start[h]],
                dst_ref=gathered.at[h, g_me],
                send_sem=out_send.at[h],
                recv_sem=out_recv.at[h],
                device_id={"group": lax.rem(g_me + k, n_group)},
                device_id_type=MESH,
            ).start()
        pltpu.make_async_copy(
            grads.at[h, start[h]], gathered.at[h, g_me], out_recv.at[h]
        ).start()
    small_ref[...] = small_acc[stages]

    leaving = (n_dom - 1) * peer_slots + (n_group - 1) * cross_slots
    for sweep in range(SWEEPS):
        for c in range(CHUNKS):
            whole = send.at[sweep, c, pl.ds(0, leaving)]
            pltpu.make_async_copy(whole, whole, send_sem.at[sweep, c]).wait()
    for s in range(stages):
        small_copies[s].wait_send()
        for h in range(CHUNKS):
            copies[h][s].wait_send()
    units = grad_ref.shape[1] // CHUNKS
    for h in range(CHUNKS):
        pltpu.make_async_copy(gathered.at[h], gathered.at[h], out_recv.at[h]).wait()
        rest = gathered.at[h, pl.ds(0, n_group - 1)]
        pltpu.make_async_copy(rest, rest, out_send.at[h]).wait()
        for g in range(n_group):
            grad_ref[g * share:(g + 1) * share, h * units:(h + 1) * units] = gathered[h, g]


def local(
    n_group, n_dom,
    features,
    known_mask,
    local_tile,
    peer_tile,
    cross_tile,
    peer_rows,
    cross_rows,
    labels,
    first_weight,
    first_bias,
    second_weight,
    second_bias,
):
    rows, width = features.shape
    units = first_weight.shape[1]
    classes = second_weight.shape[1]
    peer_slots, cross_slots = peer_rows.shape[3], cross_rows.shape[3]
    listed = jnp.concatenate([peer_rows.reshape(-1), cross_rows.reshape(-1)])
    halo_rows = listed.shape[0]
    pick = (listed[:, None] == jnp.arange(rows, dtype=jnp.int32)[None, :]).astype(jnp.bfloat16)
    blocks = n_group * n_dom
    stages = blocks.bit_length() - 1
    share = width // blocks
    cols = width // CHUNKS
    small_rows = -(-(classes + 2) // 8) * 8
    vmem = pl.BlockSpec(memory_space=pltpu.VMEM)
    f32, bf16 = jnp.float32, jnp.bfloat16
    dma = pltpu.SemaphoreType.DMA
    imputed, grad_first, small = pl.pallas_call(
        functools.partial(
            kernel, n_group, n_dom, peer_slots, cross_slots, rows * blocks
        ),
        out_shape=(
            jax.ShapeDtypeStruct((rows, width), f32),
            jax.ShapeDtypeStruct((width // n_dom, units), f32),
            jax.ShapeDtypeStruct((small_rows, units), f32),
        ),
        in_specs=[vmem] * 7 + [pl.BlockSpec(memory_space=pl.ANY)] + [vmem] * 3,
        out_specs=(vmem,) * 3,
        scratch_shapes=[
            pltpu.VMEM((width, units), bf16),
            pltpu.VMEM((CHUNKS, rows, cols), f32),
            pltpu.VMEM((SWEEPS, CHUNKS, halo_rows, cols), f32),
            pltpu.VMEM((SWEEPS, CHUNKS, halo_rows, cols), f32),
            pltpu.VMEM((rows, width), bf16),
            pltpu.VMEM((CHUNKS, blocks, share, units // CHUNKS), f32),
            pltpu.VMEM((CHUNKS, blocks, share, units // CHUNKS), f32),
            pltpu.VMEM((stages + 1, small_rows, units), f32),
            pltpu.VMEM((stages, small_rows, units), f32),
            pltpu.VMEM((CHUNKS, n_group, share, units // CHUNKS), f32),
            dma(()),
            dma((SWEEPS, CHUNKS)),
            dma((SWEEPS, CHUNKS)),
            dma((CHUNKS, stages)),
            dma((CHUNKS, stages)),
            dma((stages,)),
            dma((stages,)),
            dma((CHUNKS,)),
            dma((CHUNKS,)),
        ],
        compiler_params=pltpu.CompilerParams(
            collective_id=0, has_side_effects=True, vmem_limit_bytes=60 * 1024 * 1024
        ),
    )(
        features, known_mask[:, None], local_tile, peer_tile, cross_tile, pick, labels[:, None],
        first_weight, first_bias[None, :], second_weight, second_bias[None, :],
    )
    grad_second = small[:classes].T
    return (imputed, grad_first, small[classes], grad_second, small[classes + 1, :classes])


def solution(mesh):
    in_specs = (
        P(("group", "dom"), None),
        P(("group", "dom")),
        P(("group", "dom"), None),
        P(("group", "dom"), None),
        P(("group", "dom"), None),
        P("group", "dom", None, None),
        P("group", "dom", None, None),
        P(("group", "dom")),
        P(),
        P(),
        P(),
        P(),
    )
    out_specs = (P(("group", "dom"), None), P("dom", None), P(), P(), P())
    body = functools.partial(local, mesh.shape["group"], mesh.shape["dom"])
    return jax.shard_map(body, mesh=mesh, in_specs=in_specs, out_specs=out_specs, check_vma=False)
```

```python
import functools
import math

import jax
import jax.numpy as jnp
from jax import lax
from jax.experimental import pallas as pl
from jax.experimental.pallas import tpu as pltpu
from jax.sharding import PartitionSpec as P

SWEEPS = 3
CHUNKS = 2
MESH = pl.DeviceIdType.MESH


def split(x):
    high = x.astype(jnp.bfloat16)
    low = (x - high.astype(jnp.float32)).astype(jnp.bfloat16)
    return high, low


def two_pass(a, parts):
    out = jnp.dot(a, parts[0], preferred_element_type=jnp.float32)
    return out + jnp.dot(a, parts[1], preferred_element_type=jnp.float32)


def bits_of(name, n):
    return [(name, b) for b in range(n.bit_length() - 1)]


def reduce_orders(n_group, n_dom):
    group, dom = bits_of("group", n_group), bits_of("dom", n_dom)
    bulk_a = group + dom
    bulk_b = group[:1] + dom[:1] + group[1:] + dom[1:]
    bulk_c = group[:1] + dom[1:] + group[1:] + dom[:1]
    small = dom[1:] + group[:1] + dom[:1] + group[1:]
    return [bulk_a, bulk_b, bulk_c], small


def column(row, rows):
    shape = (rows, rows)
    diagonal = lax.broadcasted_iota(jnp.int32, shape, 0) == lax.broadcasted_iota(jnp.int32, shape, 1)
    spread = jnp.broadcast_to(row.astype(jnp.float32), shape)
    return jnp.sum(jnp.where(diagonal, spread, jnp.float32(0.0)), axis=1, keepdims=True)


def kernel(
    n_group, n_dom, peer_slots, cross_slots, total_nodes,
    feat_ref, keep_ref, local_ref, peer_ref, cross_ref, peer_list, cross_list, label_ref,
    w1_hbm, b1_ref, w2_ref, b2_ref,
    imputed_ref, grad_ref, bias1_ref, second_ref, bias2_ref,
    w1_ref, cur, send, recv, inputs, lists, grads, incoming, small_acc, small_in, gathered,
    w1_sem, send_sem, recv_sem, bulk_send, bulk_recv, small_send, small_recv,
    out_send, out_recv,
):
    sizes = {"group": n_group, "dom": n_dom}
    me = {name: lax.axis_index(name) for name in sizes}
    rows, width = feat_ref.shape
    cols = width // CHUNKS
    peer_total = n_dom * peer_slots

    load_w1 = pltpu.make_async_copy(w1_hbm, w1_ref, w1_sem)
    load_w1.start()
    barrier = pltpu.get_barrier_semaphore()

    def bit(name, b):
        return lax.rem(lax.div(me[name], 1 << b), 2)

    def flipped(name, mask):
        there = me[name]
        for b in range(mask.bit_length()):
            if (mask >> b) & 1:
                there = there + (1 << b) * (1 - 2 * bit(name, b))
        return there

    for name, n in sizes.items():
        for k in range(1, n):
            pl.semaphore_signal(
                barrier, inc=1, device_id={name: flipped(name, k)}, device_id_type=MESH
            )

    local = local_ref[...]
    halo = jnp.concatenate([peer_ref[...], cross_ref[...]], axis=1)
    degree = (
        1.0
        + jnp.sum(local.astype(jnp.float32), axis=1, keepdims=True)
        + jnp.sum(halo.astype(jnp.float32), axis=1, keepdims=True)
    )
    keep = column(keep_ref[...], rows) > 0.5
    lists[...] = jnp.zeros(lists.shape, jnp.float32)
    lists[:n_dom, :peer_slots] = peer_list[...].astype(jnp.float32)
    lists[n_dom:n_dom + n_group, :cross_slots] = cross_list[...].astype(jnp.float32)
    turned = lists[...].T.astype(jnp.int32)
    pick = []
    for q in range(n_dom + n_group):
        slots = peer_slots if q < n_dom else cross_slots
        number = lax.broadcasted_iota(jnp.int32, (slots, rows), 1)
        pick.append((turned[:slots, q:q + 1] == number).astype(jnp.float32))
    pick = jnp.concatenate(pick, axis=0).astype(jnp.bfloat16)

    def exchange(sweep, c, parts):
        out = send.at[sweep, c]
        into = recv.at[sweep, c]
        send[sweep, c] = two_pass(pick, parts)
        bases = {"dom": (0, peer_slots), "group": (peer_total, cross_slots)}
        far = [("dom", k) for k in range(n_dom // 2, n_dom)]
        near = [("group", k) for k in range(n_group - 1, 0, -1)]
        near += [("dom", k) for k in range(n_dom // 2 - 1, 0, -1)]
        for name, k in far + near:
            base, slots = bases[name]
            mine = pl.ds(pl.multiple_of(base + me[name] * slots, slots), slots)
            there = flipped(name, k)
            pltpu.make_async_remote_copy(
                src_ref=out.at[pl.ds(pl.multiple_of(base + there * slots, slots), slots)],
                dst_ref=into.at[mine],
                send_sem=send_sem.at[sweep, c],
                recv_sem=recv_sem.at[sweep, c],
                device_id={name: there},
                device_id_type=MESH,
            ).start()
        for name, (base, slots) in bases.items():
            mine = pl.ds(pl.multiple_of(base + me[name] * slots, slots), slots)
            pltpu.make_async_copy(out.at[mine], into.at[mine], recv_sem.at[sweep, c]).start()

    for c in range(CHUNKS):
        now = jnp.where(keep, feat_ref[:, c * cols:(c + 1) * cols], jnp.float32(0.0))
        cur[c] = now
        if c == 0:
            pl.semaphore_wait(barrier, n_dom - 1 + n_group - 1)
        exchange(0, c, split(now))
    pre = b1_ref[...]
    for sweep in range(SWEEPS):
        if sweep + 1 == SWEEPS:
            load_w1.wait()
        for c in range(CHUNKS):
            area = slice(c * cols, (c + 1) * cols)
            now = cur[c]
            summed = now + two_pass(local, split(now))
            pltpu.make_async_copy(
                recv.at[sweep, c], recv.at[sweep, c], recv_sem.at[sweep, c]
            ).wait()
            summed = summed + two_pass(halo, split(recv[sweep, c]))
            now = jnp.where(keep, feat_ref[:, area], summed / degree)
            if sweep + 1 < SWEEPS:
                cur[c] = now
                exchange(sweep + 1, c, split(now))
            else:
                imputed_ref[:, area] = now
                inputs[area, :] = now.T.astype(jnp.bfloat16)
                pre = pre + jnp.dot(
                    now.astype(jnp.bfloat16), w1_ref[area, :], preferred_element_type=jnp.float32
                )

    sigma = jax.nn.sigmoid(pre)
    active = (pre * sigma).astype(jnp.bfloat16)
    w2 = w2_ref[...]
    logits = b2_ref[...] + lax.dot_general(
        active, w2, (((1,), (1,)), ((), ())), preferred_element_type=jnp.float32
    )
    shifted = logits - jnp.max(logits, axis=1, keepdims=True)
    expo = jnp.exp(shifted)
    probs = expo / jnp.sum(expo, axis=1, keepdims=True)
    classes = w2.shape[0]
    label = column(label_ref[...], rows).astype(jnp.int32)
    hot = label == lax.broadcasted_iota(jnp.int32, (rows, classes), 1)
    dlogits = (probs - hot.astype(jnp.float32)) / jnp.float32(math.sqrt(total_nodes))
    dlogits_b = dlogits.astype(jnp.bfloat16)
    back = jnp.dot(dlogits_b, w2, preferred_element_type=jnp.float32)
    dpre32 = back * sigma * (1.0 + pre * (1.0 - sigma))
    dpre = dpre32.astype(jnp.bfloat16)

    orders, small_order = reduce_orders(n_group, n_dom)
    stages = len(small_order)

    def partner(name, b):
        return {name: flipped(name, 1 << b)}

    small_acc[0] = jnp.zeros(small_acc.shape[1:], jnp.float32)
    small_acc[0, :classes] = lax.dot_general(
        dlogits_b, active, (((0,), (0,)), ((), ())), preferred_element_type=jnp.float32
    )
    small_acc[0, classes:classes + 1] = jnp.sum(dpre.astype(jnp.float32), axis=0, keepdims=True)
    small_acc[0, classes + 1:classes + 2, :classes] = jnp.sum(dlogits, axis=0, keepdims=True)

    def small_copy(s):
        return pltpu.make_async_remote_copy(
            src_ref=small_acc.at[s],
            dst_ref=small_in.at[s],
            send_sem=small_send.at[s],
            recv_sem=small_recv.at[s],
            device_id=partner(*small_order[s]),
            device_id_type=MESH,
        )

    deep, share = width // n_dom, width // n_dom // n_group
    blocks = n_group * n_dom

    def place(order, where):
        at = 0
        for name, b in order:
            at = 2 * at + ((where[name] >> b) & 1)
        return at

    parts, lanes = grads.shape[0], grads.shape[3]
    orders = [orders[h % len(orders)] for h in range(parts)]
    start = [0] * parts
    copies = [[] for _ in range(parts)]

    def bulk_start(s, h):
        half = blocks >> (s + 1)
        name, b = orders[h][s]
        mine = bit(name, b)
        copy = pltpu.make_async_remote_copy(
            src_ref=grads.at[h, pl.ds(start[h] + (1 - mine) * half, half)],
            dst_ref=incoming.at[h, pl.ds(blocks - 2 * half, half)],
            send_sem=bulk_send.at[h, s],
            recv_sem=bulk_recv.at[h, s],
            device_id=partner(name, b),
            device_id_type=MESH,
        )
        copy.start()
        copies[h].append(copy)
        start[h] = start[h] + mine * half

    small_copies = [small_copy(0)]
    small_copies[0].start()
    together = max(1, 256 // lanes)
    for first in range(0, parts, together):
        group_of = range(first, first + together)
        term = jnp.dot(
            inputs[...], dpre[:, first * lanes:(first + together) * lanes],
            preferred_element_type=jnp.float32,
        )
        for h in group_of:
            for d in range(n_dom):
                for g in range(n_group):
                    top = (d * n_group + g) * share
                    grads[h, place(orders[h], {"group": g, "dom": d})] = term[
                        top:top + share, (h - first) * lanes:(h - first + 1) * lanes
                    ]
            bulk_start(0, h)

    group_bits = bits_of("group", n_group)
    my_place = 0
    for name, b in group_bits:
        my_place = 2 * my_place + bit(name, b)
    rounds = [[] for _ in range(parts)]

    def share_out(r, h):
        name, b = group_bits[len(group_bits) - 1 - r]
        held = pl.ds(lax.div(my_place, 1 << r) * (1 << r), 1 << r)
        copy = pltpu.make_async_remote_copy(
            src_ref=gathered.at[h, held],
            dst_ref=gathered.at[h, held],
            send_sem=out_send.at[h, r],
            recv_sem=out_recv.at[h, r],
            device_id=partner(name, b),
            device_id_type=MESH,
        )
        copy.start()
        rounds[h].append(copy)

    for s in range(stages):
        half = blocks >> (s + 1)
        for h in range(parts):
            copies[h][s].wait_recv()
            kept = pl.ds(start[h], half)
            total = grads[h, kept] + incoming[h, pl.ds(blocks - 2 * half, half)]
            if s + 1 < stages:
                grads[h, kept] = total
                bulk_start(s + 1, h)
            else:
                gathered[h, pl.ds(my_place, 1)] = total
                share_out(0, h)
        small_copies[s].wait_recv()
        small_acc[s + 1] = small_acc[s] + small_in[s]
        if s + 1 < stages:
            small_copies.append(small_copy(s + 1))
            small_copies[-1].start()
    second_ref[...] = small_acc[stages, :classes]
    bias1_ref[...] = small_acc[stages, classes:classes + 1]
    bias2_ref[...] = small_acc[stages, classes + 1:classes + 2, :classes]
    for r in range(len(group_bits)):
        for h in range(parts):
            rounds[h][r].wait_recv()
            if r + 1 < len(group_bits):
                share_out(r + 1, h)
    for h in range(parts):
        for g in range(n_group):
            grad_ref[g * share:(g + 1) * share, h * lanes:(h + 1) * lanes] = gathered[
                h, place(group_bits, {"group": g})
            ]

    leaving = (n_dom - 1) * peer_slots + (n_group - 1) * cross_slots
    for sweep in range(SWEEPS):
        for c in range(CHUNKS):
            whole = send.at[sweep, c, pl.ds(0, leaving)]
            pltpu.make_async_copy(whole, whole, send_sem.at[sweep, c]).wait()
    for s in range(stages):
        small_copies[s].wait_send()
        for h in range(parts):
            copies[h][s].wait_send()
    for h in range(parts):
        for copy in rounds[h]:
            copy.wait_send()


def finish(count, *refs):
    sems = refs[-1]
    copies = [
        pltpu.make_async_copy(refs[i], refs[count + i], sems.at[i]) for i in range(count)
    ]
    for copy in copies:
        copy.start()
    for copy in copies:
        copy.wait()


def local(
    n_group, n_dom,
    features,
    known_mask,
    local_tile,
    peer_tile,
    cross_tile,
    peer_rows,
    cross_rows,
    labels,
    first_weight,
    first_bias,
    second_weight,
    second_bias,
):
    rows, width = features.shape
    units = first_weight.shape[1]
    classes = second_weight.shape[1]
    peer_slots, cross_slots = peer_rows.shape[3], cross_rows.shape[3]
    halo_rows = n_dom * peer_slots + n_group * cross_slots
    blocks = n_group * n_dom
    stages = blocks.bit_length() - 1
    share = width // blocks
    cols = width // CHUNKS
    small_rows = -(-(classes + 2) // 8) * 8
    vmem = pl.BlockSpec(memory_space=pltpu.VMEM)
    f32, bf16 = jnp.float32, jnp.bfloat16
    dma = pltpu.SemaphoreType.DMA
    parts = 8 if share % 8 == 0 else 2
    list_shape = (-(-(n_dom + n_group) // 128) * 128, -(-max(peer_slots, cross_slots) // 128) * 128)
    bulk = pltpu.VMEM((parts, blocks, share, units // parts), f32)
    rounds = n_group.bit_length() - 1
    shapes = (
        jax.ShapeDtypeStruct((rows, width), f32),
        jax.ShapeDtypeStruct((width // n_dom, units), f32),
        jax.ShapeDtypeStruct((1, units), f32),
        jax.ShapeDtypeStruct((classes, units), f32),
        jax.ShapeDtypeStruct((1, classes), f32),
    )
    results = pl.pallas_call(
        functools.partial(
            kernel, n_group, n_dom, peer_slots, cross_slots, rows * blocks
        ),
        out_shape=shapes,
        in_specs=[vmem] * 8 + [pl.BlockSpec(memory_space=pl.ANY)] + [vmem] * 3,
        out_specs=(vmem,) * 5,
        scratch_shapes=[
            pltpu.VMEM((width, units), bf16),
            pltpu.VMEM((CHUNKS, rows, cols), f32),
            pltpu.VMEM((SWEEPS, CHUNKS, halo_rows, cols), f32),
            pltpu.VMEM((SWEEPS, CHUNKS, halo_rows, cols), f32),
            pltpu.VMEM((width, rows), bf16),
            pltpu.VMEM(list_shape, f32),
            bulk,
            bulk,
            pltpu.VMEM((stages + 1, small_rows, units), f32),
            pltpu.VMEM((stages, small_rows, units), f32),
            pltpu.VMEM((parts, n_group, share, units // parts), f32),
            dma(()),
            dma((SWEEPS, CHUNKS)),
            dma((SWEEPS, CHUNKS)),
            dma((parts, stages)),
            dma((parts, stages)),
            dma((stages,)),
            dma((stages,)),
            dma((parts, rounds)),
            dma((parts, rounds)),
        ],
        compiler_params=pltpu.CompilerParams(
            collective_id=0, has_side_effects=True, vmem_limit_bytes=60 * 1024 * 1024
        ),
    )(
        features, known_mask[None, :], local_tile, peer_tile, cross_tile,
        peer_rows.reshape(n_dom, peer_slots), cross_rows.reshape(n_group, cross_slots),
        labels[None, :], first_weight, first_bias[None, :], second_weight.T, second_bias[None, :],
    )
    imputed, grad_first, bias1, second, bias2 = pl.pallas_call(
        functools.partial(finish, len(shapes)),
        out_shape=shapes,
        in_specs=[pl.BlockSpec(memory_space=pl.ANY)] * len(shapes),
        out_specs=(vmem,) * len(shapes),
        scratch_shapes=[dma((len(shapes),))],
    )(*results)
    return (imputed, grad_first, bias1[0], second.T, bias2[0])


def solution(mesh):
    in_specs = (
        P(("group", "dom"), None),
        P(("group", "dom")),
        P(("group", "dom"), None),
        P(("group", "dom"), None),
        P(("group", "dom"), None),
        P("group", "dom", None, None),
        P("group", "dom", None, None),
        P(("group", "dom")),
        P(),
        P(),
        P(),
        P(),
    )
    out_specs = (P(("group", "dom"), None), P("dom", None), P(), P(), P())
    body = functools.partial(local, mesh.shape["group"], mesh.shape["dom"])
    return jax.shard_map(body, mesh=mesh, in_specs=in_specs, out_specs=out_specs, check_vma=False)
```
